32 devices in a mesh: seq: 16 (over z, x, core), tp: 2 (over y).
Axes of the slice: x: 2, y: 2, z: 4, core: 2. Of those that a mesh axis runs over, the one named last changes fastest.
Arguments:
- normed_input: bfloat16 [2048, 4096], P(('seq', 'tp')), may hold values from -6 to 6
- output_gradient: bfloat16 [2048, 14336], P('seq', 'tp'), may hold values from -0.75 to 0.75
- adapter_down: bfloat16 [64, 16, 4096], P('seq', None, 'tp'), may hold values from -0.09375 to 0.09375
- adapter_up: bfloat16 [64, 16, 14336], P('seq', None, 'tp'), may hold values from -1.5 to 1.5
- adapter_of_block: int32 [16], P('seq'), may hold values from 0 to 63
- live_per_block: int32 [16], P('seq'), may hold values from 32 to 128, as said below
- adapter_home_row: int32 [64], replicated, may hold values from 0 to 63, each once
Outputs:
- adapter_output: bfloat16 [2048, 14336], P('seq', 'tp')
- input_gradient: bfloat16 [2048, 4096], P(('seq', 'tp'))
- down_gradient: float32 [64, 16, 4096], P('seq', None, 'tp')
- up_gradient: float32 [64, 16, 14336], P('seq', None, 'tp')
The draws below stay inside these ranges and needn't reach their ends.
Inputs may be any that keep to these rules, and one draw needn't show every extreme that they name: `live_per_block`: every eighth block, counting from block 0, is full. `adapter_home_row`: each row appears once.
All inputs are finite; a program needn't handle non-finite values.
Results may differ from the reference program's by a relative error of at most 0.0051.
Values may be sent and summed in bfloat16 or wider, within the bound.
A program may use at most 128 MiB of HBM per device.

```python
import math
import jax
import jax.numpy as jnp
import numpy as np
from jax import lax

INPUT_FEATURES = 4096
HIDDEN_UNITS = 14336
ADAPTER_RANK = 16
ADAPTER_COUNT = 64
BLK = 128
TOKENS = 2048
NBLK = 16


def draw_live_per_block(key, part):
    spread = jax.random.randint(key, (NBLK,), BLK // 4, BLK + 1)
    full_rows = jnp.arange(NBLK) % 8 == 0
    return jnp.where(full_rows, BLK, spread).astype(jnp.int32)


def touch_ends(drawn, rng, least, top_value):
    dims = drawn.shape
    index_at = [jax.random.randint(jax.random.fold_in(rng, axis), (), 0, dims[axis]) for axis in range(len(dims))]
    drawn = drawn.at[tuple(index_at)].set(least)
    longest = dims.index(max(dims))
    index_at[longest] = (index_at[longest] + 1) % dims[longest]
    return drawn.at[tuple(index_at)].set(top_value)


def steps_of(stream_key, shape, pieces, least, largest):
    def one(axis_at, blocks):
        heights = jax.random.uniform(jax.random.fold_in(jax.random.fold_in(stream_key, 6), axis_at), (blocks,), jnp.float32, least / len(pieces), largest / len(pieces))
        return jnp.repeat(jnp.exp(heights), shape[axis_at] // blocks).reshape((-1,) + (1,) * (len(shape) - axis_at - 1))

    level = one(*pieces[0])
    for cut in pieces[1:]:
        level = level * one(*cut)
    return level


def rank_table(count, skew):
    loads = [(1 << 20) // math.isqrt(rank ** skew) + 1 for rank in range(1, count + 1)]
    deviation = 1 + sum(loads) // (1 << 30)
    return np.cumsum(np.array([max(1, weight // deviation) for weight in loads]))


def ranked_ids(stream_key, extent, amount, slope):
    table = rank_table(amount, slope)
    pick = jax.random.randint(jax.random.fold_in(stream_key, 1), extent, 0, int(table[amount - 1]))
    rank = jnp.searchsorted(jnp.asarray(table, jnp.int32), pick, side="right")
    return jax.random.permutation(jax.random.fold_in(stream_key, 2), amount)[rank].astype(jnp.int32)


def normal_values(key, shape, width, most, cuts=(), kind=jnp.bfloat16):
    values = jax.random.normal(key, shape, jnp.float32) * width
    if len(cuts) > 0:
        values = steps_of(key, shape, cuts, -0.22, 0.18) * values
    return jnp.clip(values, min=-most, max=most).astype(kind)


def setup_inputs(seed: int = 0) -> dict:
    splits = jax.random.split(jax.random.key(seed), 8)
    return {
        "normed_input": normal_values(splits[0], (TOKENS, INPUT_FEATURES), 1.0, 6.0, ((0, 32),)),
        "output_gradient": normal_values(splits[1], (TOKENS, HIDDEN_UNITS), 0.125, 0.75, ((0, 16), (1, 2))),
        "adapter_down": normal_values(splits[2], (ADAPTER_COUNT, ADAPTER_RANK, INPUT_FEATURES), INPUT_FEATURES ** -0.5, 0.09375, ((0, 16), (2, 2))),
        "adapter_up": normal_values(splits[3], (ADAPTER_COUNT, ADAPTER_RANK, HIDDEN_UNITS), ADAPTER_RANK ** -0.5, 1.5, ((0, 16), (2, 2))),
        "adapter_of_block": touch_ends(ranked_ids(splits[4], (NBLK,), ADAPTER_COUNT, 2), jax.random.fold_in(splits[4], 3), 0, ADAPTER_COUNT - 1).astype(jnp.int32),
        "live_per_block": draw_live_per_block(jax.random.fold_in(splits[7], 71), 0),
        "adapter_home_row": jax.random.permutation(splits[6], ADAPTER_COUNT).astype(jnp.int32),
    }


adapter_scale = 2.0


def reference(normed_input, output_gradient, adapter_down, adapter_up, adapter_of_block, live_per_block, adapter_home_row):
    total_blocks = adapter_of_block.shape[0]
    block_length = normed_input.shape[0] // total_blocks
    x_blocks = normed_input.reshape(total_blocks, block_length, normed_input.shape[1])
    g_blocks = output_gradient.reshape(total_blocks, block_length, output_gradient.shape[1])
    token_live_mask = (jnp.arange(block_length, dtype=jnp.int32)[None, :] < live_per_block[:, None]).astype(jnp.float32)

    def one_block(block_item):
        x_rows, gradient_rows, selected_adapter, mask_row = block_item
        down_factor = adapter_down[selected_adapter]
        up_factor = adapter_up[selected_adapter]
        mask_column = mask_row[:, None]
        down_sum = jnp.dot(x_rows, down_factor.T, preferred_element_type=jnp.float32)
        down_reduced = (down_sum * mask_column).astype(jnp.bfloat16)
        output_rows = (adapter_scale * jnp.dot(down_reduced, up_factor, preferred_element_type=jnp.float32)).astype(jnp.bfloat16)
        backward_total = jnp.dot(gradient_rows, up_factor.T, preferred_element_type=jnp.float32)
        backward_reduced = (adapter_scale * backward_total * mask_column).astype(jnp.bfloat16)
        gx_rows = jnp.dot(backward_reduced, down_factor, preferred_element_type=jnp.float32).astype(jnp.bfloat16)
        ga_part = jnp.dot(backward_reduced.T, x_rows, preferred_element_type=jnp.float32)
        up_gradient_piece = adapter_scale * jnp.dot(down_reduced.T, gradient_rows, preferred_element_type=jnp.float32)
        return output_rows, gx_rows, ga_part, up_gradient_piece

    up_output, gx_b, ga_b, gb_b = lax.map(one_block, (x_blocks, g_blocks, adapter_of_block, token_live_mask))
    token_count = adapter_down.shape[0]
    seg_a = jax.ops.segment_sum(ga_b, adapter_of_block, num_segments=token_count)
    seg_b = jax.ops.segment_sum(gb_b, adapter_of_block, num_segments=token_count)
    down_gradient = jnp.zeros_like(seg_a).at[adapter_home_row].set(seg_a)
    up_gradient = jnp.zeros_like(seg_b).at[adapter_home_row].set(seg_b)
    adapter_output = up_output.reshape(output_gradient.shape)
    input_gradient = gx_b.reshape(normed_input.shape)
    return adapter_output, input_gradient, down_gradient, up_gradient
```

```python
import functools

import jax
import jax.numpy as jnp
from jax import lax
from jax.experimental import pallas as pl
from jax.experimental.pallas import tpu as pltpu
from jax.sharding import PartitionSpec as P

adapter_scale = 2.0
GROUP = 4
MESH = pl.DeviceIdType.MESH
VMEM = pltpu.VMEM


def pieces(width, most):
    tiles = width // 128
    count = max(k for k in range(1, most + 1) if tiles % k == 0)
    step = width // count
    return [(i * step, step) for i in range(count)]


def greet(n, tp, me, mine):
    barrier = pltpu.get_barrier_semaphore()

    def seq_signal(d, carry):
        pl.semaphore_signal(barrier, inc=1, device_id=(lax.rem(me + d, n), mine), device_id_type=MESH)
        return carry

    lax.fori_loop(1, n, seq_signal, 0)
    for d in range(1, tp):
        pl.semaphore_signal(barrier, inc=1, device_id=(me, lax.rem(mine + d, tp)), device_id_type=MESH)
    pl.semaphore_wait(barrier, n - 1 + tp - 1)


def factor_kernel(
    n, tp, a_ref, b_ref, x_ref, id_ref,
    a_out, b_out, x_out, id_out,
    fa, fb, sa, sb, za, zb,
    raw_send, raw_recv, z_send, z_recv, id_send, id_recv, x_send, x_recv,
):
    me, mine = lax.axis_index("seq"), lax.axis_index("tp")
    planes = n // GROUP
    plane, spot = me // GROUP, lax.rem(me, GROUP)
    near = me + 1 - 2 * lax.rem(spot, 2)
    far = me + 2 - 4 * (spot // 2)
    far_spot = spot + 2 - 4 * (spot // 2)
    rows = a_ref.shape[0]
    rank = a_out.shape[0]
    total = fa.shape[0]
    width = x_out.shape[2]
    greet(n, tp, me, mine)

    def remote(src, dst, send, recv, seq_at, tp_at):
        return pltpu.make_async_remote_copy(
            src_ref=src, dst_ref=dst, send_sem=send, recv_sem=recv,
            device_id=(seq_at, tp_at), device_id_type=MESH,
        )

    def id_copy(d):
        return remote(id_ref, id_out.at[me], id_send.at[d], id_recv.at[d], lax.rem(me + d, n), mine)

    lax.fori_loop(1, n, lambda d, c: (id_copy(d).start(), c)[1], 0)

    cuts = [(a_ref, fa, sa, za, a_out, *cut) for cut in pieces(a_ref.shape[1], 2)]
    cuts += [(b_ref, fb, sb, zb, b_out, *cut) for cut in pieces(b_ref.shape[1], 7)]
    own = pl.ds(pl.multiple_of(spot * rows, rows), rows)
    other = pl.ds(pl.multiple_of(far_spot * rows, rows), rows)
    to_far, to_near, forward = [], [], []
    for j, (src, full, _, _, _, start, size) in enumerate(cuts):
        cols = pl.ds(start, size)
        to_far.append(remote(src.at[:, cols], full.at[own, cols], raw_send.at[0, j], raw_recv.at[0, j], far, mine))
        to_near.append(remote(src.at[:, cols], full.at[own, cols], raw_send.at[1, j], raw_recv.at[1, j], near, mine))
        forward.append(remote(full.at[other, cols], full.at[other, cols], raw_send.at[2, j], raw_recv.at[2, j], near, mine))
        to_far[j].start()
        to_near[j].start()
    x_copies = []
    for d in range(1, tp):
        peer = lax.rem(mine + d, tp)
        copy = remote(
            x_ref.at[:, pl.ds(pl.multiple_of(peer * width, width), width)], x_out.at[mine],
            x_send.at[d], x_recv.at[d], me, peer,
        )
        copy.start()
        x_copies.append(copy)
    x_out[mine] = x_ref[:, pl.ds(pl.multiple_of(mine * width, width), width)]
    id_out[me] = id_ref[...]
    fa[own, :] = a_ref[...]
    fb[own, :] = b_ref[...]
    lax.fori_loop(1, n, lambda d, c: (id_copy(d).wait(), c)[1], 0)

    base = plane * (total // rank)
    row_at = lax.broadcasted_iota(jnp.int32, (rank, total), 0)
    col_at = lax.broadcasted_iota(jnp.int32, (rank, total), 1)
    picks = []
    for p in range(planes):
        wanted = jnp.broadcast_to(id_out[p * GROUP + spot, 0:1, 0:1], (rank, total)) - base
        picks.append((col_at == wanted * rank + row_at).astype(jnp.float32))
    pick = jnp.concatenate(picks, axis=0).astype(jnp.bfloat16)

    z_copies = []
    for j, (_, full, chosen, landed, _, start, size) in enumerate(cuts):
        cols = pl.ds(start, size)
        to_far[j].wait_recv()
        forward[j].start()
        to_near[j].wait_recv()
        forward[j].wait_recv()
        got = jnp.dot(pick, full[:, cols], preferred_element_type=jnp.float32).astype(jnp.bfloat16)
        chosen[:, :, cols] = got.reshape(planes, rank, size)
        for d in range(1, planes):
            to = lax.rem(plane + d, planes)
            copy = remote(
                chosen.at[to, :, cols], landed.at[d, :, cols],
                z_send.at[d, j], z_recv.at[d, j], to * GROUP + spot, mine,
            )
            copy.start()
            z_copies.append(copy)
    for j, (_, _, chosen, landed, out, start, size) in enumerate(cuts):
        cols = pl.ds(start, size)
        value = chosen[plane, :, cols].astype(jnp.float32)
        for d in range(1, planes):
            z_copies[j * (planes - 1) + d - 1].wait_recv()
            value += landed[d, :, cols].astype(jnp.float32)
        out[:, cols] = value.astype(jnp.bfloat16)
    for copy in x_copies:
        copy.wait()
    for copy in to_far + to_near + forward + z_copies:
        copy.wait_send()


def fetch_factors(n, tp, a, b, x, ids):
    slots, rank, width = a.shape
    hidden = b.shape[2]
    tokens = x.shape[0]
    planes = n // GROUP
    cuts = len(pieces(width, 2)) + len(pieces(hidden, 7))
    total = GROUP * slots * rank
    low = jnp.bfloat16
    dma = pltpu.SemaphoreType.DMA
    return pl.pallas_call(
        functools.partial(factor_kernel, n, tp),
        out_shape=(
            jax.ShapeDtypeStruct((rank, width), low),
            jax.ShapeDtypeStruct((rank, hidden), low),
            jax.ShapeDtypeStruct((tp, tokens, width), low),
            jax.ShapeDtypeStruct((n, 8, 128), jnp.int32),
        ),
        in_specs=[pl.BlockSpec(memory_space=VMEM)] * 4,
        out_specs=(pl.BlockSpec(memory_space=VMEM),) * 4,
        scratch_shapes=[
            VMEM((total, width), low), VMEM((total, hidden), low),
            VMEM((planes, rank, width), low), VMEM((planes, rank, hidden), low),
            VMEM((planes, rank, width), low), VMEM((planes, rank, hidden), low),
            dma((3, cuts)), dma((3, cuts)), dma((planes, cuts)), dma((planes, cuts)),
            dma((n,)), dma((n,)), dma((tp,)), dma((tp,)),
        ],
        compiler_params=pltpu.CompilerParams(
            collective_id=0, has_side_effects=True, vmem_limit_bytes=48 * 1024 * 1024
        ),
    )(a.reshape(slots * rank, width), b.reshape(slots * rank, hidden), x, ids)


def gradient_kernel(
    n, tp, ga_ref, gb_ref, gx_ref, place_ref,
    a_out, b_out, x_out,
    fa, fb,
    z_send, z_recv, far_send, far_recv, x_send, x_recv,
):
    me, mine = lax.axis_index("seq"), lax.axis_index("tp")
    planes = n // GROUP
    plane, spot = me // GROUP, lax.rem(me, GROUP)
    near = me + 1 - 2 * lax.rem(spot, 2)
    far = me + 2 - 4 * (spot // 2)
    far_spot = spot + 2 - 4 * (spot // 2)
    rank = ga_ref.shape[0]
    width = gx_ref.shape[2]
    column = planes * rank
    greet(n, tp, me, mine)

    def remote(src, dst, send, recv, seq_at, tp_at):
        return pltpu.make_async_remote_copy(
            src_ref=src, dst_ref=dst, send_sem=send, recv_sem=recv,
            device_id=(seq_at, tp_at), device_id_type=MESH,
        )

    cuts = [(gb_ref, fb, b_out, *cut) for cut in pieces(gb_ref.shape[1], 7)]
    cuts += [(ga_ref, fa, a_out, *cut) for cut in pieces(ga_ref.shape[1], 2)]
    row = spot * column + plane * rank
    slot = pl.ds(pl.multiple_of(row, rank), rank)
    own = pl.ds(pl.multiple_of(spot * column, column), column)
    other = pl.ds(pl.multiple_of(far_spot * column, column), column)
    z_copies, to_far, to_near, forward = [], [], [], []
    for j, (src, full, _, start, size) in enumerate(cuts):
        cols = pl.ds(start, size)
        for d in range(1, planes):
            copy = remote(
                src.at[:, cols], full.at[slot, cols], z_send.at[d, j], z_recv.at[d, j],
                lax.rem(plane + d, planes) * GROUP + spot, mine,
            )
            copy.start()
            z_copies.append(copy)
    x_copies = []
    for d in range(1, tp):
        peer = lax.rem(mine + d, tp)
        copy = remote(
            gx_ref.at[peer], x_out.at[:, pl.ds(pl.multiple_of(mine * width, width), width)],
            x_send.at[d], x_recv.at[d], me, peer,
        )
        copy.start()
        x_copies.append(copy)
    x_out[:, pl.ds(pl.multiple_of(mine * width, width), width)] = gx_ref[mine]
    fa[slot, :] = ga_ref[...]
    fb[slot, :] = gb_ref[...]

    def finish(j):
        _, full, out, start, size = cuts[j]
        cols = pl.ds(start, size)
        to_near[j].wait_recv()
        forward[j].wait_recv()
        out[:, cols] = jnp.dot(place_ref[...], full[:, cols], preferred_element_type=jnp.float32)

    def pass_on(j):
        to_far[j].wait_recv()
        forward[j].start()

    for j, (src, full, out, start, size) in enumerate(cuts):
        cols = pl.ds(start, size)
        for d in range(1, planes):
            z_copies[j * (planes - 1) + d - 1].wait_recv()
        to_far.append(remote(full.at[own, cols], full.at[own, cols], far_send.at[0, j], far_recv.at[0, j], far, mine))
        to_near.append(remote(full.at[own, cols], full.at[own, cols], far_send.at[1, j], far_recv.at[1, j], near, mine))
        forward.append(remote(full.at[other, cols], full.at[other, cols], far_send.at[2, j], far_recv.at[2, j], near, mine))
        to_far[j].start()
        to_near[j].start()
        if j >= 1:
            pass_on(j - 1)
        if j >= 2:
            finish(j - 2)
    last = len(cuts) - 1
    pass_on(last)
    finish(last - 1)
    finish(last)
    for copy in x_copies:
        copy.wait()
    for copy in to_far + to_near + forward + z_copies:
        copy.wait_send()


def deliver_gradients(n, tp, ga, gb, gx, place):
    rank, width = ga.shape
    hidden = gb.shape[1]
    tokens = gx.shape[1]
    planes = n // GROUP
    cuts = len(pieces(width, 2)) + len(pieces(hidden, 7))
    total = n * rank
    mine = place.shape[0]
    low = jnp.bfloat16
    dma = pltpu.SemaphoreType.DMA
    return pl.pallas_call(
        functools.partial(gradient_kernel, n, tp),
        out_shape=(
            jax.ShapeDtypeStruct((mine, width), jnp.float32),
            jax.ShapeDtypeStruct((mine, hidden), jnp.float32),
            jax.ShapeDtypeStruct((tokens, tp * width), low),
        ),
        in_specs=[pl.BlockSpec(memory_space=VMEM)] * 4,
        out_specs=(pl.BlockSpec(memory_space=VMEM),) * 3,
        scratch_shapes=[
            VMEM((total, width), low), VMEM((total, hidden), low),
            dma((planes, cuts)), dma((planes, cuts)), dma((3, cuts)), dma((3, cuts)),
            dma((tp,)), dma((tp,)),
        ],
        compiler_params=pltpu.CompilerParams(
            collective_id=1, has_side_effects=True, vmem_limit_bytes=48 * 1024 * 1024
        ),
    )(ga, gb, gx, place)


def per_device(
    normed_input,
    output_gradient,
    adapter_down,
    adapter_up,
    adapter_of_block,
    live_per_block,
    adapter_home_row,
):
    n, tp = lax.axis_size("seq"), lax.axis_size("tp")
    slots, rank, width = adapter_down.shape
    hidden = adapter_up.shape[2]
    token_rows = output_gradient.shape[0]
    adapters = adapter_home_row.shape[0]
    planes = n // GROUP
    f32, low = jnp.float32, jnp.bfloat16
    ids = jnp.broadcast_to(adapter_of_block[0], (8, 128))
    pick_a, pick_b, x, all_ids = fetch_factors(n, tp, adapter_down, adapter_up, normed_input, ids)
    x = x.reshape(token_rows, width)
    g = output_gradient

    block_ids = all_ids[:, 0, 0]
    chosen = block_ids[:, None] == jnp.arange(adapters, dtype=jnp.int32)[None, :]
    block_row = jnp.sum(jnp.where(chosen, adapter_home_row[None, :], 0), axis=1)
    block_row = block_row.reshape(planes, GROUP).T.reshape(n)
    out_at = jnp.arange(slots * rank, dtype=jnp.int32)
    in_at = jnp.arange(n * rank, dtype=jnp.int32)
    my_row = lax.axis_index("seq") * slots + out_at // rank
    place = (
        (jnp.repeat(block_row, rank)[None, :] == my_row[:, None])
        & ((in_at % rank)[None, :] == (out_at % rank)[:, None])
    ).astype(low)

    part = jnp.concatenate(
        [
            jnp.einsum("rd,td->rt", pick_a, x, preferred_element_type=f32),
            jnp.einsum("rf,tf->rt", pick_b, g, preferred_element_type=f32),
        ],
        axis=0,
    )
    both = part
    for d in range(1, tp):
        both = both + lax.ppermute(part, "tp", [(i, (i + d) % tp) for i in range(tp)])
    live = (jnp.arange(token_rows, dtype=jnp.int32) < live_per_block[0]).astype(f32)[None, :]
    down = (both[:rank] * live).astype(low)
    back = (adapter_scale * both[rank:] * live).astype(low)
    gb = (adapter_scale * jnp.dot(down, g, preferred_element_type=f32)).astype(low)
    ga = jnp.dot(back, x, preferred_element_type=f32).astype(low)
    gx = jnp.einsum("rt,rd->td", back, pick_a, preferred_element_type=f32).astype(low)
    out = (adapter_scale * jnp.einsum("rt,rf->tf", down, pick_b, preferred_element_type=f32)).astype(low)
    grad_a, grad_b, gx = deliver_gradients(n, tp, ga, gb, gx.reshape(tp, token_rows // tp, width), place)
    return (out, gx, grad_a.reshape(slots, rank, width), grad_b.reshape(slots, rank, hidden))


def solution(mesh):
    placed = (
        P(("seq", "tp"), None),
        P("seq", "tp"),
        P("seq", None, "tp"),
        P("seq", None, "tp"),
        P("seq"),
        P("seq"),
        P(),
    )
    return jax.shard_map(
        per_device,
        mesh=mesh,
        in_specs=placed,
        out_specs=(
            P("seq", "tp"),
            P(("seq", "tp"), None),
            P("seq", None, "tp"),
            P("seq", None, "tp"),
        ),
        check_vma=False,
    )
```

```python
import functools

import jax
import jax.numpy as jnp
from jax import lax
from jax.experimental import pallas as pl
from jax.experimental.pallas import tpu as pltpu
from jax.sharding import PartitionSpec as P

adapter_scale = 2.0
GROUP = 4
MESH = pl.DeviceIdType.MESH
VMEM = pltpu.VMEM


def pieces(width, most):
    tiles = width // 128
    count = max(k for k in range(1, most + 1) if tiles % k == 0)
    step = width // count
    return [(i * step, step) for i in range(count)]


def greet(n, tp, me, mine):
    barrier = pltpu.get_barrier_semaphore()

    def seq_signal(d, carry):
        pl.semaphore_signal(barrier, inc=1, device_id=(lax.rem(me + d, n), mine), device_id_type=MESH)
        return carry

    lax.fori_loop(1, n, seq_signal, 0)
    for d in range(1, tp):
        pl.semaphore_signal(barrier, inc=1, device_id=(me, lax.rem(mine + d, tp)), device_id_type=MESH)
    pl.semaphore_wait(barrier, n - 1 + tp - 1)


def step_kernel(
    n, tp, a_ref, b_ref, x_ref, g_ref, id_ref, live_ref,
    down_out, b_out, grad_a, grad_b, x_out,
    fa, fb, sa, sb, za, zb, ga, gb, pick_a, xt, g, ids, part, gx,
    raw_send, raw_recv, z_send, z_recv, grad_send, grad_recv, far_send, far_recv,
    id_send, id_recv, x_send, x_recv, part_send, part_recv, gx_send, gx_recv, local_sem,
):
    me, mine = lax.axis_index("seq"), lax.axis_index("tp")
    planes = n // GROUP
    plane, spot = me // GROUP, lax.rem(me, GROUP)
    near = me + 1 - 2 * lax.rem(spot, 2)
    far = me + 2 - 4 * (spot // 2)
    far_spot = spot + 2 - 4 * (spot // 2)
    rows = a_ref.shape[0]
    rank = pick_a.shape[0]
    total = fa.shape[0]
    width = xt.shape[2]
    tokens = g.shape[0]
    slots = rows // rank
    column = planes * rank
    f32, low = jnp.float32, jnp.bfloat16

    def remote(src, dst, send, recv, seq_at, tp_at):
        return pltpu.make_async_remote_copy(
            src_ref=src, dst_ref=dst, send_sem=send, recv_sem=recv,
            device_id=(seq_at, tp_at), device_id_type=MESH,
        )

    def columns(index):
        return pl.ds(pl.multiple_of(index * width, width), width)

    own = pl.ds(pl.multiple_of(spot * rows, rows), rows)
    other = pl.ds(pl.multiple_of(far_spot * rows, rows), rows)
    local = [
        pltpu.make_async_copy(a_ref, fa.at[own, :], local_sem.at[0]),
        pltpu.make_async_copy(b_ref, fb.at[own, :], local_sem.at[1]),
        pltpu.make_async_copy(x_ref.at[:, columns(mine)], xt.at[mine], local_sem.at[2]),
        pltpu.make_async_copy(g_ref, g, local_sem.at[3]),
    ]
    for copy in local:
        copy.start()
    greet(n, tp, me, mine)

    def id_copy(d):
        return remote(id_ref, ids.at[me], id_send.at[d], id_recv.at[d], lax.rem(me + d, n), mine)

    lax.fori_loop(1, n, lambda d, c: (id_copy(d).start(), c)[1], 0)

    a_cuts, b_cuts = pieces(a_ref.shape[1], 2), pieces(b_ref.shape[1], 7)
    cuts = [(a_ref, fa, sa, za, *cut) for cut in a_cuts] + [(b_ref, fb, sb, zb, *cut) for cut in b_cuts]
    to_far, to_near, forward = [], [], []
    for j, (src, full, _, _, start, size) in enumerate(cuts):
        cols = pl.ds(start, size)
        to_far.append(remote(src.at[:, cols], full.at[own, cols], raw_send.at[0, j], raw_recv.at[0, j], far, mine))
        to_near.append(remote(src.at[:, cols], full.at[own, cols], raw_send.at[1, j], raw_recv.at[1, j], near, mine))
        forward.append(remote(full.at[other, cols], full.at[other, cols], raw_send.at[2, j], raw_recv.at[2, j], near, mine))
        to_far[j].start()
        to_near[j].start()
    x_copies = []
    for d in range(1, tp):
        peer = lax.rem(mine + d, tp)
        x_copies.append(remote(x_ref.at[:, columns(peer)], xt.at[mine], x_send.at[d], x_recv.at[d], me, peer))
        x_copies[-1].start()
    ids[me] = id_ref[...]
    for copy in local:
        copy.wait()
    lax.fori_loop(1, n, lambda d, c: (id_copy(d).wait(), c)[1], 0)

    base = plane * (total // rank)
    row_at = lax.broadcasted_iota(jnp.int32, (rank, total), 0)
    col_at = lax.broadcasted_iota(jnp.int32, (rank, total), 1)
    picks = []
    for p in range(planes):
        wanted = jnp.broadcast_to(ids[p * GROUP + spot, 0:1, 0:1], (rank, total)) - base
        picks.append((col_at == wanted * rank + row_at).astype(f32))
    pick = jnp.concatenate(picks, axis=0).astype(low)
    place_row = lax.broadcasted_iota(jnp.int32, (rows, n * rank), 0)
    place_col = lax.broadcasted_iota(jnp.int32, (rows, n * rank), 1)
    target = jnp.full((rows, n * rank), -1, jnp.int32)
    for p in range(planes):
        for q in range(GROUP):
            first = (q * planes + p) * rank
            home = jnp.broadcast_to(ids[p * GROUP + q, 1:2, 0:1], (rows, n * rank))
            at = (home - me * slots) * rank + place_col - first
            target = jnp.where((place_col >= first) & (place_col < first + rank), at, target)
    place = (target == place_row).astype(f32).astype(low)

    z_copies = []

    def choose(j):
        _, full, chosen, landed, start, size = cuts[j]
        cols = pl.ds(start, size)
        to_far[j].wait_recv()
        forward[j].start()
        to_near[j].wait_recv()
        forward[j].wait_recv()
        got = jnp.dot(pick, full[:, cols], preferred_element_type=f32).astype(low)
        chosen[:, :, cols] = got.reshape(planes, rank, size)
        for d in range(1, planes):
            to = lax.rem(plane + d, planes)
            copy = remote(
                chosen.at[to, :, cols], landed.at[d, :, cols],
                z_send.at[d, j], z_recv.at[d, j], to * GROUP + spot, mine,
            )
            copy.start()
            z_copies.append(copy)

    def settle(j, out):
        _, _, chosen, landed, start, size = cuts[j]
        cols = pl.ds(start, size)
        value = chosen[plane, :, cols].astype(f32)
        for d in range(1, planes):
            z_copies[j * (planes - 1) + d - 1].wait_recv()
            value += landed[d, :, cols].astype(f32)
        out[:, cols] = value.astype(low)

    def outer(left, right):
        return lax.dot_general(left, right, (((1,), (1,)), ((), ())), preferred_element_type=f32)

    part_copies = []

    def share(which, value):
        part[which, 0] = value
        for d in range(1, tp):
            copy = remote(
                part.at[which, 0], part.at[which, d], part_send.at[which, d], part_recv.at[which, d],
                me, lax.rem(mine + d, tp),
            )
            copy.start()
            part_copies.append(copy)

    def collect(which):
        value = part[which, 0]
        for d in range(1, tp):
            part_copies[which * (tp - 1) + d - 1].wait_recv()
            value = value + part[which, d]
        return value * live_ref[0:1, :]

    grads = [(gb, grad_b, *cut) for cut in b_cuts] + [(ga, grad_a, *cut) for cut in a_cuts]
    slot = pl.ds(pl.multiple_of(spot * column + plane * rank, rank), rank)
    mine_all = pl.ds(pl.multiple_of(spot * column, column), column)
    other_all = pl.ds(pl.multiple_of(far_spot * column, column), column)
    count = len(grads)
    spread_copies = [[] for _ in range(count)]
    far_copies, near_copies, pass_copies = [], [], []

    def spread(j):
        full, _, start, size = grads[j]
        cols = pl.ds(start, size)
        for d in range(1, planes):
            copy = remote(
                full.at[slot, cols], full.at[slot, cols], grad_send.at[d, j], grad_recv.at[d, j],
                lax.rem(plane + d, planes) * GROUP + spot, mine,
            )
            copy.start()
            spread_copies[j].append(copy)

    def cross(j):
        full, _, start, size = grads[j]
        cols = pl.ds(start, size)
        for copy in spread_copies[j]:
            copy.wait_recv()
        far_copies.append(remote(full.at[mine_all, cols], full.at[mine_all, cols], far_send.at[0, j], far_recv.at[0, j], far, mine))
        near_copies.append(remote(full.at[mine_all, cols], full.at[mine_all, cols], far_send.at[1, j], far_recv.at[1, j], near, mine))
        pass_copies.append(remote(full.at[other_all, cols], full.at[other_all, cols], far_send.at[2, j], far_recv.at[2, j], near, mine))
        far_copies[j].start()
        near_copies[j].start()

    def pass_on(j):
        far_copies[j].wait_recv()
        pass_copies[j].start()

    def finish(j):
        full, out, start, size = grads[j]
        cols = pl.ds(start, size)
        near_copies[j].wait_recv()
        pass_copies[j].wait_recv()
        out[:, cols] = jnp.dot(place, full[:, cols], preferred_element_type=f32)

    na, nb = len(a_cuts), len(b_cuts)
    for j in range(na + 2):
        choose(j)
    for j in range(na):
        settle(j, pick_a)
    for copy in x_copies:
        copy.wait()
    x_all = xt[...].reshape(tokens, width)
    share(0, outer(pick_a[...], x_all))
    choose(na + 2)
    down = collect(0).astype(low)
    down_out[...] = down
    for start, size in b_cuts:
        cols = pl.ds(start, size)
        gb[slot, cols] = (adapter_scale * jnp.dot(down, g[:, cols], preferred_element_type=f32)).astype(low)
    sent = 0
    for j in range(na + 3, na + nb):
        spread(sent)
        sent += 1
        choose(j)
    crossed = 0
    early = min(2, sent)
    for j in range(early):
        cross(j)
    crossed = early
    spread(sent)
    sent += 1
    total_back = jnp.zeros((rank, tokens), f32)
    for j in range(nb):
        settle(na + j, b_out)
        cols = pl.ds(*b_cuts[j])
        total_back = total_back + outer(b_out[:, cols], g[:, cols])
    share(1, total_back)
    while sent < nb:
        spread(sent)
        sent += 1
    while crossed < min(nb, 4):
        cross(crossed)
        crossed += 1
    back_full = adapter_scale * collect(1)
    back = back_full.astype(low)
    ga[slot, :] = jnp.dot(back, x_all, preferred_element_type=f32).astype(low)
    for j in range(nb, count):
        spread(j)
    back_t = back_full.T.astype(low)
    gx[...] = jnp.dot(back_t, pick_a[...], preferred_element_type=f32).astype(low).reshape(gx.shape)
    gx_copies = []
    for d in range(1, tp):
        peer = lax.rem(mine + d, tp)
        gx_copies.append(remote(gx.at[peer], x_out.at[:, columns(mine)], gx_send.at[d], gx_recv.at[d], me, peer))
        gx_copies[-1].start()
    x_out[:, columns(mine)] = gx[mine]
    passed, done = 0, 0
    while done < count:
        if crossed < count:
            cross(crossed)
            crossed += 1
        if passed < count and passed < crossed - (1 if crossed < count else 0):
            pass_on(passed)
            passed += 1
        if crossed == count:
            while passed < count and passed - done < 2:
                pass_on(passed)
                passed += 1
            finish(done)
            done += 1
        elif done < passed - 1:
            finish(done)
            done += 1
    for copy in gx_copies:
        copy.wait()
    for copy in to_far + to_near + forward + z_copies + part_copies:
        copy.wait_send()
    for group in spread_copies + [far_copies, near_copies, pass_copies]:
        for copy in group:
            copy.wait_send()


def step(n, tp, a, b, x, g, ids, live):
    slots, rank, width = a.shape
    hidden = b.shape[2]
    rows = x.shape[0]
    tokens = g.shape[0]
    planes = n // GROUP
    cuts = len(pieces(width, 2)) + len(pieces(hidden, 7))
    total = GROUP * slots * rank
    low, f32 = jnp.bfloat16, jnp.float32
    dma = pltpu.SemaphoreType.DMA
    anywhere = pl.BlockSpec(memory_space=pl.ANY)
    inside = pl.BlockSpec(memory_space=VMEM)
    return pl.pallas_call(
        functools.partial(step_kernel, n, tp),
        out_shape=(
            jax.ShapeDtypeStruct((rank, tokens), low),
            jax.ShapeDtypeStruct((rank, hidden), low),
            jax.ShapeDtypeStruct((slots * rank, width), f32),
            jax.ShapeDtypeStruct((slots * rank, hidden), f32),
            jax.ShapeDtypeStruct((rows, tp * width), low),
        ),
        in_specs=[anywhere] * 4 + [inside] * 2,
        out_specs=(inside,) * 5,
        scratch_shapes=[
            VMEM((total, width), low), VMEM((total, hidden), low),
            VMEM((planes, rank, width), low), VMEM((planes, rank, hidden), low),
            VMEM((planes, rank, width), low), VMEM((planes, rank, hidden), low),
            VMEM((n * rank, width), low), VMEM((n * rank, hidden), low),
            VMEM((rank, width), low), VMEM((tp, rows, width), low), VMEM((tokens, hidden), low),
            VMEM((n, 8, 128), jnp.int32), VMEM((2, tp, rank, tokens), f32), VMEM((tp, rows, width), low),
            dma((3, cuts)), dma((3, cuts)), dma((planes, cuts)), dma((planes, cuts)),
            dma((planes, cuts)), dma((planes, cuts)), dma((3, cuts)), dma((3, cuts)),
            dma((n,)), dma((n,)), dma((tp,)), dma((tp,)), dma((2, tp)), dma((2, tp)),
            dma((tp,)), dma((tp,)), dma((4,)),
        ],
        compiler_params=pltpu.CompilerParams(
            collective_id=0, has_side_effects=True, vmem_limit_bytes=56 * 1024 * 1024
        ),
    )(a.reshape(slots * rank, width), b.reshape(slots * rank, hidden), x, g, ids, live)


def per_device(
    normed_input,
    output_gradient,
    adapter_down,
    adapter_up,
    adapter_of_block,
    live_per_block,
    adapter_home_row,
):
    n, tp = lax.axis_size("seq"), lax.axis_size("tp")
    slots, rank, width = adapter_down.shape
    hidden = adapter_up.shape[2]
    tokens = output_gradient.shape[0]
    adapters = adapter_home_row.shape[0]
    f32, low = jnp.float32, jnp.bfloat16
    adapter = adapter_of_block[0]
    home = jnp.sum(jnp.where(jnp.arange(adapters, dtype=jnp.int32) == adapter, adapter_home_row, 0))
    ids = jnp.where(jnp.arange(8, dtype=jnp.int32)[:, None] == 0, adapter, home)
    ids = jnp.broadcast_to(ids, (8, 128))
    live = (jnp.arange(tokens, dtype=jnp.int32) < live_per_block[0]).astype(f32)
    live = jnp.broadcast_to(live[None, :], (8, tokens))
    down, pick_b, grad_a, grad_b, gx = step(
        n, tp, adapter_down, adapter_up, normed_input, output_gradient, ids, live
    )
    out = (adapter_scale * jnp.einsum("rt,rf->tf", down, pick_b, preferred_element_type=f32)).astype(low)
    return (out, gx, grad_a.reshape(slots, rank, width), grad_b.reshape(slots, rank, hidden))


def solution(mesh):
    placed = (
        P(("seq", "tp"), None),
        P("seq", "tp"),
        P("seq", None, "tp"),
        P("seq", None, "tp"),
        P("seq"),
        P("seq"),
        P(),
    )
    return jax.shard_map(
        per_device,
        mesh=mesh,
        in_specs=placed,
        out_specs=(
            P("seq", "tp"),
            P(("seq", "tp"), None),
            P("seq", None, "tp"),
            P("seq", None, "tp"),
        ),
        check_vma=False,
    )
```

```python
import functools

import jax
import jax.numpy as jnp
from jax import lax
from jax.experimental import pallas as pl
from jax.experimental.pallas import tpu as pltpu
from jax.sharding import PartitionSpec as P

adapter_scale = 2.0
GROUP = 4
MESH = pl.DeviceIdType.MESH
VMEM = pltpu.VMEM


def pieces(width, most):
    tiles = width // 128
    count = max(k for k in range(1, most + 1) if tiles % k == 0)
    step = width // count
    return [(i * step, step) for i in range(count)]


def greet(n, tp, me, mine):
    barrier = pltpu.get_barrier_semaphore()

    def seq_signal(d, carry):
        pl.semaphore_signal(barrier, inc=1, device_id=(lax.rem(me + d, n), mine), device_id_type=MESH)
        return carry

    lax.fori_loop(1, n, seq_signal, 0)
    for d in range(1, tp):
        pl.semaphore_signal(barrier, inc=1, device_id=(me, lax.rem(mine + d, tp)), device_id_type=MESH)
    pl.semaphore_wait(barrier, n - 1 + tp - 1)


def step_kernel(
    n, tp, a_ref, b_ref, x_ref, g_ref, id_ref, live_ref,
    down_out, b_out, grad_a, grad_b, x_out,
    fa, fb, sa, sb, za, zb, ga, gb, pick_a, xt, g, ids, part, gx,
    raw_send, raw_recv, z_send, z_recv, grad_send, grad_recv, far_send, far_recv,
    id_send, id_recv, x_send, x_recv, part_send, part_recv, gx_send, gx_recv, local_sem,
):
    me, mine = lax.axis_index("seq"), lax.axis_index("tp")
    planes = n // GROUP
    plane, spot = me // GROUP, lax.rem(me, GROUP)
    near = me + 1 - 2 * lax.rem(spot, 2)
    far = me + 2 - 4 * (spot // 2)
    far_spot = spot + 2 - 4 * (spot // 2)
    rows = a_ref.shape[0]
    rank = pick_a.shape[0]
    total = fa.shape[0]
    width = xt.shape[2]
    tokens = g.shape[0]
    slots = rows // rank
    column = planes * rank
    f32, low = jnp.float32, jnp.bfloat16

    def remote(src, dst, send, recv, seq_at, tp_at):
        return pltpu.make_async_remote_copy(
            src_ref=src, dst_ref=dst, send_sem=send, recv_sem=recv,
            device_id=(seq_at, tp_at), device_id_type=MESH,
        )

    def columns(index):
        return pl.ds(pl.multiple_of(index * width, width), width)

    own = pl.ds(pl.multiple_of(spot * rows, rows), rows)
    other = pl.ds(pl.multiple_of(far_spot * rows, rows), rows)
    local = [
        pltpu.make_async_copy(a_ref, fa.at[own, :], local_sem.at[0]),
        pltpu.make_async_copy(b_ref, fb.at[own, :], local_sem.at[1]),
        pltpu.make_async_copy(x_ref.at[:, columns(mine)], xt.at[mine], local_sem.at[2]),
        pltpu.make_async_copy(g_ref, g, local_sem.at[3]),
    ]
    for copy in local:
        copy.start()
    greet(n, tp, me, mine)

    def id_copy(d):
        return remote(id_ref, ids.at[me], id_send.at[d], id_recv.at[d], lax.rem(me + d, n), mine)

    lax.fori_loop(1, n, lambda d, c: (id_copy(d).start(), c)[1], 0)

    a_cuts, b_cuts = pieces(a_ref.shape[1], 2), pieces(b_ref.shape[1], 7)
    cuts = [(a_ref, fa, sa, za, *cut) for cut in a_cuts] + [(b_ref, fb, sb, zb, *cut) for cut in b_cuts]
    to_far, to_near, forward = [], [], []
    for j, (src, full, _, _, start, size) in enumerate(cuts):
        cols = pl.ds(start, size)
        to_far.append(remote(src.at[:, cols], full.at[own, cols], raw_send.at[0, j], raw_recv.at[0, j], far, mine))
        to_near.append(remote(src.at[:, cols], full.at[own, cols], raw_send.at[1, j], raw_recv.at[1, j], near, mine))
        forward.append(remote(full.at[other, cols], full.at[other, cols], raw_send.at[2, j], raw_recv.at[2, j], near, mine))
        to_far[j].start()
        to_near[j].start()
    x_copies = []
    for d in range(1, tp):
        peer = lax.rem(mine + d, tp)
        x_copies.append(remote(x_ref.at[:, columns(peer)], xt.at[mine], x_send.at[d], x_recv.at[d], me, peer))
        x_copies[-1].start()
    ids[me] = id_ref[...]
    for copy in local:
        copy.wait()
    lax.fori_loop(1, n, lambda d, c: (id_copy(d).wait(), c)[1], 0)

    base = plane * (total // rank)
    row_at = lax.broadcasted_iota(jnp.int32, (rank, total), 0)
    col_at = lax.broadcasted_iota(jnp.int32, (rank, total), 1)
    picks = []
    for p in range(planes):
        wanted = jnp.broadcast_to(ids[p * GROUP + spot, 0:1, 0:1], (rank, total)) - base
        picks.append((col_at == wanted * rank + row_at).astype(f32))
    pick = jnp.concatenate(picks, axis=0).astype(low)
    place_row = lax.broadcasted_iota(jnp.int32, (rows, n * rank), 0)
    place_col = lax.broadcasted_iota(jnp.int32, (rows, n * rank), 1)
    target = jnp.full((rows, n * rank), -1, jnp.int32)
    for p in range(planes):
        for q in range(GROUP):
            first = (q * planes + p) * rank
            home = jnp.broadcast_to(ids[p * GROUP + q, 1:2, 0:1], (rows, n * rank))
            at = (home - me * slots) * rank + place_col - first
            target = jnp.where((place_col >= first) & (place_col < first + rank), at, target)
    place = (target == place_row).astype(f32).astype(low)

    z_copies = []

    def choose(j):
        _, full, chosen, landed, start, size = cuts[j]
        cols = pl.ds(start, size)
        to_far[j].wait_recv()
        forward[j].start()
        to_near[j].wait_recv()
        forward[j].wait_recv()
        got = jnp.dot(pick, full[:, cols], preferred_element_type=f32).astype(low)
        chosen[:, :, cols] = got.reshape(planes, rank, size)
        for d in range(1, planes):
            to = lax.rem(plane + d, planes)
            copy = remote(
                chosen.at[to, :, cols], landed.at[d, :, cols],
                z_send.at[d, j], z_recv.at[d, j], to * GROUP + spot, mine,
            )
            copy.start()
            z_copies.append(copy)

    def settle(j, out):
        _, _, chosen, landed, start, size = cuts[j]
        cols = pl.ds(start, size)
        value = chosen[plane, :, cols].astype(f32)
        for d in range(1, planes):
            z_copies[j * (planes - 1) + d - 1].wait_recv()
            value += landed[d, :, cols].astype(f32)
        out[:, cols] = value.astype(low)

    def outer(left, right):
        return lax.dot_general(left, right, (((1,), (1,)), ((), ())), preferred_element_type=f32)

    part_copies = []

    def share(which, value):
        part[which, 0] = value
        for d in range(1, tp):
            copy = remote(
                part.at[which, 0], part.at[which, d], part_send.at[which, d], part_recv.at[which, d],
                me, lax.rem(mine + d, tp),
            )
            copy.start()
            part_copies.append(copy)

    def collect(which):
        value = part[which, 0]
        for d in range(1, tp):
            part_copies[which * (tp - 1) + d - 1].wait_recv()
            value = value + part[which, d]
        return value * live_ref[0:1, :]

    grads = [(gb, grad_b, *cut) for cut in b_cuts] + [(ga, grad_a, *cut) for cut in a_cuts]
    slot = pl.ds(pl.multiple_of(spot * column + plane * rank, rank), rank)
    mine_all = pl.ds(pl.multiple_of(spot * column, column), column)
    other_all = pl.ds(pl.multiple_of(far_spot * column, column), column)
    count = len(grads)
    far_copies, near_copies, pass_copies = [], [], []

    def hop(source, side, j):
        full, _, start, size = grads[j]
        at = pl.ds(pl.multiple_of(spot * column + source * rank, rank), rank)
        view = full.at[at, pl.ds(start, size)]
        to = lax.rem(plane + (1 if side == 0 else planes - 1), planes)
        return remote(view, view, grad_send.at[2 * source + side, j], grad_recv.at[source, j], to * GROUP + spot, mine)

    def spread(j):
        @pl.when(plane < planes - 1)
        def _():
            hop(plane, 0, j).start()

        @pl.when(plane > 0)
        def _():
            hop(plane, 1, j).start()

    def relay(j):
        for d in range(1, planes):
            @pl.when(plane >= d)
            def _():
                hop(plane - d, 0, j).wait_recv()

                @pl.when(plane < planes - 1)
                def _():
                    hop(plane - d, 0, j).start()

            @pl.when(plane + d < planes)
            def _():
                hop(plane + d, 1, j).wait_recv()

                @pl.when(plane > 0)
                def _():
                    hop(plane + d, 1, j).start()

    def relay_end(j):
        for d in range(planes):
            @pl.when((plane >= d) & (plane < planes - 1))
            def _():
                hop(plane - d, 0, j).wait_send()

            @pl.when((plane + d < planes) & (plane > 0))
            def _():
                hop(plane + d, 1, j).wait_send()

    def cross(j):
        full, _, start, size = grads[j]
        cols = pl.ds(start, size)
        relay(j)
        far_copies.append(remote(full.at[mine_all, cols], full.at[mine_all, cols], far_send.at[0, j], far_recv.at[0, j], far, mine))
        near_copies.append(remote(full.at[mine_all, cols], full.at[mine_all, cols], far_send.at[1, j], far_recv.at[1, j], near, mine))
        pass_copies.append(remote(full.at[other_all, cols], full.at[other_all, cols], far_send.at[2, j], far_recv.at[2, j], near, mine))
        far_copies[j].start()
        near_copies[j].start()

    def pass_on(j):
        far_copies[j].wait_recv()
        pass_copies[j].start()

    def finish(j):
        full, out, start, size = grads[j]
        cols = pl.ds(start, size)
        near_copies[j].wait_recv()
        pass_copies[j].wait_recv()
        out[:, cols] = jnp.dot(place, full[:, cols], preferred_element_type=f32)

    na, nb = len(a_cuts), len(b_cuts)
    for j in range(na + 2):
        choose(j)
    for j in range(na):
        settle(j, pick_a)
    for copy in x_copies:
        copy.wait()
    x_all = xt[...].reshape(tokens, width)
    share(0, outer(pick_a[...], x_all))
    choose(na + 2)
    down = collect(0).astype(low)
    down_out[...] = down
    for start, size in b_cuts:
        cols = pl.ds(start, size)
        gb[slot, cols] = (adapter_scale * jnp.dot(down, g[:, cols], preferred_element_type=f32)).astype(low)
    sent = 0
    for j in range(na + 3, na + nb):
        spread(sent)
        sent += 1
        choose(j)
    crossed = 0
    early = min(2, sent)
    for j in range(early):
        cross(j)
    crossed = early
    spread(sent)
    sent += 1
    total_back = jnp.zeros((rank, tokens), f32)
    for j in range(nb):
        settle(na + j, b_out)
        cols = pl.ds(*b_cuts[j])
        total_back = total_back + outer(b_out[:, cols], g[:, cols])
    share(1, total_back)
    while sent < nb:
        spread(sent)
        sent += 1
    while crossed < min(nb, 4):
        cross(crossed)
        crossed += 1
    back_full = adapter_scale * collect(1)
    back = back_full.astype(low)
    ga[slot, :] = jnp.dot(back, x_all, preferred_element_type=f32).astype(low)
    for j in range(nb, count):
        spread(j)
    back_t = back_full.T.astype(low)
    gx[...] = jnp.dot(back_t, pick_a[...], preferred_element_type=f32).astype(low).reshape(gx.shape)
    gx_copies = []
    for d in range(1, tp):
        peer = lax.rem(mine + d, tp)
        gx_copies.append(remote(gx.at[peer], x_out.at[:, columns(mine)], gx_send.at[d], gx_recv.at[d], me, peer))
        gx_copies[-1].start()
    x_out[:, columns(mine)] = gx[mine]
    passed, done = 0, 0
    while done < count:
        if crossed < count:
            cross(crossed)
            crossed += 1
        if passed < count and passed < crossed - (1 if crossed < count else 0):
            pass_on(passed)
            passed += 1
        if crossed == count:
            while passed < count and passed - done < 2:
                pass_on(passed)
                passed += 1
            finish(done)
            done += 1
        elif done < passed - 1:
            finish(done)
            done += 1
    for copy in gx_copies:
        copy.wait()
    for copy in to_far + to_near + forward + z_copies + part_copies:
        copy.wait_send()
    for j in range(count):
        relay_end(j)
    for group in [far_copies, near_copies, pass_copies]:
        for copy in group:
            copy.wait_send()


def step(n, tp, a, b, x, g, ids, live):
    slots, rank, width = a.shape
    hidden = b.shape[2]
    rows = x.shape[0]
    tokens = g.shape[0]
    planes = n // GROUP
    cuts = len(pieces(width, 2)) + len(pieces(hidden, 7))
    total = GROUP * slots * rank
    low, f32 = jnp.bfloat16, jnp.float32
    dma = pltpu.SemaphoreType.DMA
    anywhere = pl.BlockSpec(memory_space=pl.ANY)
    inside = pl.BlockSpec(memory_space=VMEM)
    return pl.pallas_call(
        functools.partial(step_kernel, n, tp),
        out_shape=(
            jax.ShapeDtypeStruct((rank, tokens), low),
            jax.ShapeDtypeStruct((rank, hidden), low),
            jax.ShapeDtypeStruct((slots * rank, width), f32),
            jax.ShapeDtypeStruct((slots * rank, hidden), f32),
            jax.ShapeDtypeStruct((rows, tp * width), low),
        ),
        in_specs=[anywhere] * 4 + [inside] * 2,
        out_specs=(inside,) * 5,
        scratch_shapes=[
            VMEM((total, width), low), VMEM((total, hidden), low),
            VMEM((planes, rank, width), low), VMEM((planes, rank, hidden), low),
            VMEM((planes, rank, width), low), VMEM((planes, rank, hidden), low),
            VMEM((n * rank, width), low), VMEM((n * rank, hidden), low),
            VMEM((rank, width), low), VMEM((tp, rows, width), low), VMEM((tokens, hidden), low),
            VMEM((n, 8, 128), jnp.int32), VMEM((2, tp, rank, tokens), f32), VMEM((tp, rows, width), low),
            dma((3, cuts)), dma((3, cuts)), dma((planes, cuts)), dma((planes, cuts)),
            dma((2 * planes, cuts)), dma((planes, cuts)), dma((3, cuts)), dma((3, cuts)),
            dma((n,)), dma((n,)), dma((tp,)), dma((tp,)), dma((2, tp)), dma((2, tp)),
            dma((tp,)), dma((tp,)), dma((4,)),
        ],
        compiler_params=pltpu.CompilerParams(
            collective_id=0, has_side_effects=True, vmem_limit_bytes=56 * 1024 * 1024
        ),
    )(a.reshape(slots * rank, width), b.reshape(slots * rank, hidden), x, g, ids, live)


def per_device(
    normed_input,
    output_gradient,
    adapter_down,
    adapter_up,
    adapter_of_block,
    live_per_block,
    adapter_home_row,
):
    n, tp = lax.axis_size("seq"), lax.axis_size("tp")
    slots, rank, width = adapter_down.shape
    hidden = adapter_up.shape[2]
    tokens = output_gradient.shape[0]
    adapters = adapter_home_row.shape[0]
    f32, low = jnp.float32, jnp.bfloat16
    adapter = adapter_of_block[0]
    home = jnp.sum(jnp.where(jnp.arange(adapters, dtype=jnp.int32) == adapter, adapter_home_row, 0))
    ids = jnp.where(jnp.arange(8, dtype=jnp.int32)[:, None] == 0, adapter, home)
    ids = jnp.broadcast_to(ids, (8, 128))
    live = (jnp.arange(tokens, dtype=jnp.int32) < live_per_block[0]).astype(f32)
    live = jnp.broadcast_to(live[None, :], (8, tokens))
    down, pick_b, grad_a, grad_b, gx = step(
        n, tp, adapter_down, adapter_up, normed_input, output_gradient, ids, live
    )
    out = (adapter_scale * jnp.einsum("rt,rf->tf", down, pick_b, preferred_element_type=f32)).astype(low)
    return (out, gx, grad_a.reshape(slots, rank, width), grad_b.reshape(slots, rank, hidden))


def solution(mesh):
    placed = (
        P(("seq", "tp"), None),
        P("seq", "tp"),
        P("seq", None, "tp"),
        P("seq", None, "tp"),
        P("seq"),
        P("seq"),
        P(),
    )
    return jax.shard_map(
        per_device,
        mesh=mesh,
        in_specs=placed,
        out_specs=(
            P("seq", "tp"),
            P(("seq", "tp"), None),
            P("seq", None, "tp"),
            P("seq", None, "tp"),
        ),
        check_vma=False,
    )
```
